32 devices in a mesh: ctx: 16 (over z, x, core), head: 2 (over y).
Axes of the slice: x: 2, y: 2, z: 4, core: 2. Of those that a mesh axis runs over, the one named last changes fastest.
Arguments:
- conv_in: bfloat16 [8192, 2048], P('ctx', 'head'), may hold values from -6 to 6
- conv_weight: float32 [4, 2048], P(None, 'head'), may hold values from -3 to 3
- conv_bias: float32 [2048], P('head'), may hold values from -3 to 3
- qk_weight: bfloat16 [2, 8, 256, 256], P(None, 'head'), may hold values from -0.375 to 0.375
- value_in: bfloat16 [8192, 4096], P('ctx', 'head'), may hold values from -6 to 6
- gate_pre: float32 [2, 8, 8192], P(None, 'head', 'ctx'), may hold values from -6 to 300, as said below
- norm_gain: float32 [4096], P('head'), may hold values from 0.5 to 1.5
- out_weight: bfloat16 [4096, 4096], P('head'), may hold values from -0.125 to 0.125
Outputs:
- layer_out: bfloat16 [8192, 4096], P('ctx', 'head')
The draws below stay inside these ranges and needn't reach their ends.
Inputs may be any that keep to these rules, and one draw needn't show every extreme that they name: gate_pre[0] holds input-gate preactivations and gate_pre[1] forget-gate preactivations.
All inputs are finite; a program needn't handle non-finite values.
Results may differ from the reference program's by a relative error of at most 0.02.
Values may be sent and summed in bfloat16 or wider, within the bound.
No kernel may reach another device: no remote copies, remote signals or barrier semaphores. Data moves between devices by JAX's collectives and lax.ppermute only.
A program may use at most 192 MiB of HBM per device.

```python
import math
import jax
import jax.numpy as jnp
from jax import lax

D = 4096
HEAD_TOTAL = 8
DK = 256
DV = 512
CONV = 4
BLOCK = 512
TOK_DEV = 512
TOKEN_TOTAL = 8192
N_HEAD = 2


def draw_gate_pre(key, part):
    key_sequence = jax.random.split(key, 11)
    token_positions = jnp.arange(TOKEN_TOTAL)
    in_gate = jnp.clip(jax.random.normal(key_sequence[0], (HEAD_TOTAL, TOKEN_TOTAL), jnp.float32), -4.0, 4.0)
    slow_count = jax.random.randint(key_sequence[4], (), 3, 6)
    ranking = jax.random.permutation(key_sequence[5], HEAD_TOTAL)
    slow_heads = ranking < slow_count
    rough = jnp.exp(jax.random.uniform(key_sequence[6], (HEAD_TOTAL, TOKEN_TOTAL), jnp.float32, math.log(0.5), math.log(2.0)))
    shard_factor = jnp.exp(jax.random.uniform(key_sequence[7], (HEAD_TOTAL, TOKEN_TOTAL // TOK_DEV), jnp.float32, math.log(0.5), math.log(2.0)))
    shard_factor = jnp.repeat(shard_factor, TOK_DEV, axis=1)
    fast_rate = jnp.exp(jax.random.uniform(key_sequence[8], (HEAD_TOTAL,), jnp.float32, math.log(10.0 / TOK_DEV), math.log(17.0 / TOK_DEV)))
    base_rate = jnp.where(slow_heads, 0.5 / TOKEN_TOTAL, fast_rate)
    forget_factor = base_rate[:, None] * rough * shard_factor
    span_position = jax.random.randint(key_sequence[9], (HEAD_TOTAL, 3), 0, TOKEN_TOTAL)
    span_length = jax.random.uniform(key_sequence[10], (HEAD_TOTAL, 3), jnp.float32, 0.22, 0.69)
    for span_index in range(3):
        forget_factor = forget_factor + jnp.where(token_positions[None, :] == span_position[:, span_index:span_index + 1], span_length[:, span_index:span_index + 1], 0.0)
    forget_pre = -jnp.log(jnp.expm1(forget_factor))
    return jnp.stack([in_gate, forget_pre]).astype(jnp.float32)


def strengthened(result, key, source, target, blocks, factor):
    owner, partner = [(jnp.arange(result.shape[axis_at]) // (result.shape[axis_at] // blocks)).reshape([-1 if axis == axis_at else 1 for axis in range(result.ndim)]) for axis_at in (source, target)]
    chosen = jax.random.permutation(key, blocks)[partner]
    strong = (owner == chosen) | (owner == (partner + blocks // 2) % blocks)
    return jnp.where(strong, factor * result, result)


def shard_levels(own_key, shape, pieces, smallest, largest):
    def one(dim, shards_of):
        steps = jax.random.uniform(jax.random.fold_in(jax.random.fold_in(own_key, 6), dim), (shards_of,), jnp.float32, smallest / len(pieces), largest / len(pieces))
        return jnp.repeat(jnp.exp(steps), shape[dim] // shards_of).reshape((-1,) + (1,) * (len(shape) - dim - 1))

    factor_of = one(*pieces[0])
    for cut in pieces[1:]:
        factor_of = factor_of * one(*cut)
    return factor_of


def gaussian(stream_key, dims, deviation, most, pieces=(), dtype=jnp.bfloat16):
    drawn = jax.random.normal(stream_key, dims, jnp.float32) * deviation
    if len(pieces) > 0:
        drawn = shard_levels(stream_key, dims, pieces, -0.22, 0.18) * drawn
    return jnp.clip(drawn, min=-most, max=most).astype(dtype)


def noise_with(stream_key, dims, deviation, limit, pieces, heavy, held_as=jnp.bfloat16):
    result = deviation * jax.random.normal(stream_key, dims, jnp.float32)
    if pieces:
        result = result * shard_levels(stream_key, dims, pieces, -0.22, 0.18)
    return jnp.clip(strengthened(result, jax.random.fold_in(stream_key, 3), *heavy), -limit, limit).astype(held_as)


def setup_inputs(seed: int = 0) -> dict:
    keys = jax.random.split(jax.random.key(seed), 9)
    conv_in = gaussian(keys[0], (TOKEN_TOTAL, HEAD_TOTAL * DK), 1.0, 6.0, ((0, 16), (1, 2)))
    conv_weight = gaussian(keys[1], (CONV, HEAD_TOTAL * DK), CONV ** -0.5, 3.0, ((1, 2),), jnp.float32)
    conv_bias = gaussian(keys[2], (HEAD_TOTAL * DK,), 0.5, 3.0, ((0, 2),), jnp.float32)
    qk_weight = gaussian(keys[3], (2, HEAD_TOTAL, DK, DK), DK ** -0.5, 0.375, ((1, 2),))
    value_in = gaussian(keys[4], (TOKEN_TOTAL, HEAD_TOTAL * DV), 1.0, 6.0, ((0, 16), (1, 2)))
    gate_pre = draw_gate_pre(jax.random.fold_in(keys[8], 71), 0)
    norm_gain = jnp.clip(1.0 + 0.1 * jax.random.normal(keys[6], (HEAD_TOTAL * DV,), jnp.float32), 0.5, 1.5)
    out_weight = noise_with(keys[7], (HEAD_TOTAL * DV, D), (HEAD_TOTAL * DV) ** -0.5, 0.125, ((0, 2),), (0, 1, 2, 2.0))
    return dict(conv_in=conv_in, conv_weight=conv_weight, conv_bias=conv_bias, qk_weight=qk_weight, value_in=value_in, gate_pre=gate_pre, norm_gain=norm_gain, out_weight=out_weight)


def block_step(carry_state, block_data):
    state_mat, state_max = carry_state
    queries, key_rows, values, in_gate, log_forget = block_data
    block_len = in_gate.shape[1]
    cum_decay = jnp.cumsum(log_forget, axis=1)
    row_ids = lax.broadcasted_iota(jnp.int32, (block_len, block_len), 0)
    col_ids = lax.broadcasted_iota(jnp.int32, (block_len, block_len), 1)
    log_weight = jnp.where((row_ids >= col_ids)[None], cum_decay[:, :, None] - cum_decay[:, None, :] + in_gate[:, None, :], -jnp.inf)
    carry_log = cum_decay + state_max[:, None]
    stabilizer = jnp.maximum(lax.optimization_barrier(jnp.max(log_weight, axis=2)), carry_log)
    query_f = queries.astype(jnp.float32)
    scores = jnp.einsum('thd,shd->hts', query_f, key_rows.astype(jnp.float32), precision=lax.Precision.HIGHEST)
    weights = (scores * jnp.exp(log_weight - stabilizer[:, :, None])).astype(jnp.bfloat16)
    inner_sum = jnp.einsum('hts,shv->thv', weights.astype(jnp.float32), values.astype(jnp.float32), precision=lax.Precision.HIGHEST)
    carried = jnp.einsum('thd,hdv->thv', query_f, state_mat, precision=lax.Precision.HIGHEST)
    numerator = inner_sum + jnp.exp(carry_log - stabilizer).T[:, :, None] * carried
    block_decay = cum_decay[:, -1]
    end_log = block_decay[:, None] - cum_decay + in_gate
    new_max = jnp.maximum(state_max + block_decay, lax.optimization_barrier(jnp.max(end_log, axis=1)))
    scaled = (key_rows.astype(jnp.float32) * jnp.exp(end_log - new_max[:, None]).T[:, :, None]).astype(jnp.bfloat16)
    update = jnp.einsum('shd,shv->hdv', scaled.astype(jnp.float32), values.astype(jnp.float32), precision=lax.Precision.HIGHEST)
    state_mat = jnp.exp(state_max + block_decay - new_max)[:, None, None] * state_mat + update
    return ((state_mat, new_max), numerator)

def reference(conv_in, conv_weight, conv_bias, qk_weight, value_in, gate_pre, norm_gain, out_weight):
    total_tok = conv_in.shape[0]
    padded = jnp.concatenate([jnp.zeros((CONV - 1, conv_in.shape[1]), jnp.float32), conv_in.astype(jnp.float32)], axis=0)
    conv_pre = conv_bias + jnp.zeros((total_tok, conv_in.shape[1]), jnp.float32)
    for offset in range(CONV):
        conv_pre = conv_pre + conv_weight[offset] * padded[offset:offset + total_tok]
    activated = jax.nn.silu(conv_pre).astype(jnp.bfloat16).reshape(total_tok, HEAD_TOTAL, DK).astype(jnp.float32)
    queries = jnp.einsum('thd,hde->the', activated, qk_weight[0].astype(jnp.float32), precision=lax.Precision.HIGHEST).astype(jnp.bfloat16)
    key_rows = (jnp.einsum('thd,hde->the', activated, qk_weight[1].astype(jnp.float32), precision=lax.Precision.HIGHEST) * DK ** (-0.5)).astype(jnp.bfloat16)
    values = value_in.reshape(total_tok, HEAD_TOTAL, DV)
    in_gate = gate_pre[0]
    log_forget = jax.nn.log_sigmoid(gate_pre[1])
    num_blocks = total_tok // BLOCK
    inputs = (queries.reshape(num_blocks, BLOCK, HEAD_TOTAL, DK), key_rows.reshape(num_blocks, BLOCK, HEAD_TOTAL, DK), values.reshape(num_blocks, BLOCK, HEAD_TOTAL, DV), in_gate.reshape(HEAD_TOTAL, num_blocks, BLOCK).transpose(1, 0, 2), log_forget.reshape(HEAD_TOTAL, num_blocks, BLOCK).transpose(1, 0, 2))
    start = (jnp.zeros((HEAD_TOTAL, DK, DV), jnp.float32), jnp.full((HEAD_TOTAL,), -1e+30, jnp.float32))
    ignored, numerator = lax.scan(block_step, start, inputs)
    numerator = numerator.reshape(total_tok, HEAD_TOTAL, DV)
    scale_inv = lax.rsqrt(lax.optimization_barrier(jnp.mean(numerator * numerator, axis=2, keepdims=True)) + 1e-06)
    normed = (numerator * scale_inv * norm_gain.reshape(HEAD_TOTAL, DV)).astype(jnp.bfloat16).reshape(total_tok, HEAD_TOTAL * DV)
    group_width = HEAD_TOTAL * DV // N_HEAD
    mixed_out = jnp.zeros((total_tok, D), jnp.float32)
    for group_index in range(N_HEAD):
        lower = group_index * group_width
        part_sum = jnp.dot(normed[:, lower:lower + group_width], out_weight[lower:lower + group_width], preferred_element_type=jnp.float32).astype(jnp.bfloat16)
        mixed_out = mixed_out + lax.optimization_barrier(part_sum).astype(jnp.float32)
    return mixed_out.astype(jnp.bfloat16)
```

```python
import functools
import jax
import jax.numpy as jnp
from jax import lax
from jax.experimental import pallas as pl
from jax.experimental.pallas import tpu as pltpu
from jax.sharding import PartitionSpec as P


F32 = jnp.float32
BF16 = jnp.bfloat16
EMPTY = -1e30
TILE = 16
LANES = 128


def dot(a, b, ca, cb):
    return lax.dot_general(a, b, (((ca,), (cb,)), ((), ())), preferred_element_type=F32)


def call(kernel, n_scalar, grid, in_specs, out_specs, out_shape, scratch=(), aliases={}, cost=None):
    return pl.pallas_call(
        kernel,
        grid_spec=pltpu.PrefetchScalarGridSpec(
            num_scalar_prefetch=n_scalar,
            grid=grid,
            in_specs=in_specs,
            out_specs=out_specs,
            scratch_shapes=list(scratch),
        ),
        out_shape=out_shape,
        input_output_aliases=aliases,
        cost_estimate=cost,
    )


def sds(shape, dtype):
    return jax.ShapeDtypeStruct(shape, dtype)


def cost_of(flops, moved):
    return pl.CostEstimate(flops=int(flops), transcendentals=0, bytes_accessed=int(moved))


def whole_block(shape):
    return pl.BlockSpec(shape, lambda *_: (0,) * len(shape))


def gate_kernel(gate_ref, rows_ref, cols_ref, sums_ref):
    in_gate = gate_ref[0]
    pre = gate_ref[1]
    heads, length = in_gate.shape
    log_forget = -(jnp.maximum(-pre, 0.0) + jnp.log1p(jnp.exp(-jnp.abs(pre))))
    both = jnp.concatenate([log_forget, in_gate], axis=0)
    lane = lax.broadcasted_iota(jnp.int32, both.shape, 1)
    cum = both
    step = 1
    while step < length:
        cum = cum + jnp.where(lane >= step, pltpu.roll(cum, step, 1), 0.0)
        step *= 2
    cum = cum[:heads]
    shifted = in_gate - cum
    run = jnp.concatenate([shifted, shifted], axis=0)
    step = 1
    while step < length:
        run = jnp.maximum(run, jnp.where(lane >= step, pltpu.roll(run, step, 1), -jnp.inf))
        step *= 2
    run = run[:heads]
    decay = cum[:, length - 1 :]
    top = run[:, length - 1 :]
    rows_ref[...] = jnp.concatenate([shifted, shifted], axis=0)
    cols = jnp.concatenate([run, jnp.exp(shifted - top)], axis=0)
    cols_ref[...] = jnp.transpose(cols)
    sums = jnp.concatenate([top + decay, decay], axis=0)
    sums_ref[...] = jnp.broadcast_to(sums, (2 * heads, LANES))


def column(cols_ref, index):
    cols = cols_ref[...]
    lane = lax.broadcasted_iota(jnp.int32, cols.shape, 1)
    return jnp.sum(jnp.where(lane == index, cols, 0.0), axis=1, keepdims=True)


def state_kernel(heads, scale, ids, halo_ref, conv_ref, taps_ref, bias_ref, weight_ref, value_ref, cols_ref,
                 act_ref, key_ref, state_ref, pad):
    head = ids[0] + pl.program_id(0)
    rows = conv_ref.shape[0]
    taps = taps_ref.shape[0]
    pad[0:8, :] = halo_ref[TILE - 8 :, :].astype(F32)
    pad[8:, :] = conv_ref[...].astype(F32)
    total = bias_ref[...]
    for offset in range(taps):
        total = total + taps_ref[offset : offset + 1, :] * pad[8 - (taps - 1) + offset : 8 - (taps - 1) + offset + rows, :]
    act = (total / (1.0 + jnp.exp(-total))).astype(BF16)
    act_ref[...] = act
    keys = (dot(act, weight_ref[0, 0], 1, 0) * scale).astype(BF16)
    key_ref[...] = keys
    scaled = (keys.astype(F32) * column(cols_ref, heads + head)).astype(BF16)
    state_ref[0] = dot(scaled, value_ref[...], 0, 0).astype(BF16)


def inner_kernel(ids, act_ref, key_ref, weight_ref, value_ref, rows_ref, cols_ref, query_ref, inner_ref):
    head = ids[0] + pl.program_id(0)
    queries = dot(act_ref[...], weight_ref[0, 0], 1, 0).astype(BF16)
    query_ref[...] = queries
    scores = dot(queries, key_ref[...], 1, 1)
    row = lax.broadcasted_iota(jnp.int32, scores.shape, 0)
    col = lax.broadcasted_iota(jnp.int32, scores.shape, 1)
    log_weight = rows_ref[pl.ds(head, 1), :] - column(cols_ref, head)
    weights = scores * jnp.exp(jnp.where(row >= col, log_weight, -jnp.inf))
    inner_ref[...] = dot(weights.astype(BF16), value_ref[...], 1, 0).astype(BF16)


def split_rows(value):
    high = value.astype(BF16).astype(F32)
    rest = value - high
    middle = rest.astype(BF16).astype(F32)
    return [high, middle, rest - middle]


def scalar_tile(values):
    rows = [row for value in values for row in split_rows(value)]
    rows.append(jnp.zeros((TILE - len(rows), LANES), F32))
    return jnp.concatenate(rows, axis=0).astype(BF16)


def join_rows(tile, index):
    tile = tile.astype(F32)
    return tile[3 * index : 3 * index + 1] + tile[3 * index + 1 : 3 * index + 2] + tile[3 * index + 2 : 3 * index + 3]


def wide(row, width):
    return jnp.concatenate([row] * (width // LANES), axis=1)


def chip_kernel(chips, per, ids, own_ref, other_ref, own_sums, other_sums, *rest):
    outs, weights = rest[:chips], rest[chips]
    core, chip = ids[1], ids[2]
    half, keys, width = own_ref.shape
    heads = 2 * half
    part = half * keys // chips
    for local in range(half):
        head = core * half + local
        own_top, own_decay = own_sums[pl.ds(head, 1), :], own_sums[pl.ds(heads + head, 1), :]
        far_top, far_decay = other_sums[pl.ds(head, 1), :], other_sums[pl.ds(heads + head, 1), :]
        first = core == 0
        own_log = own_top + jnp.where(first, far_decay, 0.0)
        far_log = far_top + jnp.where(first, 0.0, own_decay)
        top = jnp.maximum(own_log, far_log)
        weights[4 * local : 4 * local + 1] = jnp.exp(own_log - top)
        weights[4 * local + 1 : 4 * local + 2] = jnp.exp(far_log - top)
        weights[4 * local + 2 : 4 * local + 3] = top
        weights[4 * local + 3 : 4 * local + 4] = own_decay + far_decay
    for k in range(chips):
        owner = lax.rem(chip + k, chips)
        local = owner // per
        start = pl.multiple_of(lax.rem(owner, per) * part, part)
        own = own_ref[local, pl.ds(start, part), :].astype(F32)
        far = other_ref[local, pl.ds(start, part), :].astype(F32)
        mine = weights[pl.ds(4 * local, 1), :]
        its = weights[pl.ds(4 * local + 1, 1), :]
        both = (wide(mine, width) * own + wide(its, width) * far).astype(BF16)
        for b in range(width // LANES):
            outs[k][b * part : (b + 1) * part, :] = both[:, b * LANES : (b + 1) * LANES]
        outs[k][width // LANES * part :, :] = scalar_tile(
            [weights[pl.ds(4 * local + 2, 1), :], weights[pl.ds(4 * local + 3, 1), :]]
        )


def owner_kernel(chips, ids, *rest):
    ins, outs, held, made = rest[:chips], rest[chips : 2 * chips], rest[2 * chips], rest[2 * chips + 1]
    chip = ids[2]
    size = ins[0].shape[0] - TILE
    for k in range(chips):
        held[k] = ins[k][...]
    total = jnp.zeros((size, LANES), F32)
    top = jnp.full((1, LANES), EMPTY, F32)
    for source in range(chips):
        slot_out = lax.rem(source - chip + chips, chips)
        slot_in = lax.rem(chip - source + chips, chips)
        made[slot_out, 0:size] = total.astype(BF16)
        made[slot_out, size:] = scalar_tile([top])
        if source < chips - 1:
            tile = held[slot_in, size:]
            new, decay = join_rows(tile, 0), join_rows(tile, 1)
            next_top = jnp.maximum(top + decay, new)
            old_weight = jnp.exp(top + decay - next_top)
            new_weight = jnp.exp(new - next_top)
            total = old_weight * total + new_weight * held[slot_in, 0:size].astype(F32)
            top = next_top
    for k in range(chips):
        outs[k][...] = made[k]


def incoming_kernel(chips, per, ids, *rest):
    ins = rest[:chips]
    own_ref, other_ref, own_sums, other_sums, keep_ref, send_ref, keep_top, send_top, tops = rest[chips:]
    core, chip = ids[1], ids[2]
    half, keys, width = own_ref.shape
    heads = 2 * half
    part = half * keys // chips
    first = core == 0
    for k in range(chips):
        owner = lax.rem(chip - k + chips, chips)
        local = owner // per
        start = pl.multiple_of(lax.rem(owner, per) * part, part)
        head = core * half + local
        top = join_rows(ins[k][width // LANES * part :, :], 0)
        tops[pl.ds(local, 1), :] = top
        near_top = jnp.where(first, own_sums[pl.ds(head, 1), :], other_sums[pl.ds(head, 1), :])
        near_decay = jnp.where(first, own_sums[pl.ds(heads + head, 1), :], other_sums[pl.ds(heads + head, 1), :])
        next_top = jnp.maximum(top + near_decay, near_top)
        old_weight = jnp.exp(top + near_decay - next_top)
        new_weight = jnp.exp(near_top - next_top)
        tops[pl.ds(4 + local, 1), :] = next_top
        for b in range(width // LANES):
            lanes = slice(b * LANES, (b + 1) * LANES)
            before = ins[k][b * part : (b + 1) * part, :]
            own = own_ref[local, pl.ds(start, part), lanes].astype(F32)
            far = other_ref[local, pl.ds(start, part), lanes].astype(F32)
            near = jnp.where(first, own, far)
            raw = before.astype(F32)
            after = old_weight * raw + new_weight * near
            keep_ref[local, pl.ds(start, part), lanes] = jnp.where(first, raw, after).astype(BF16)
            send_ref[local, pl.ds(start, part), lanes] = jnp.where(first, after, raw).astype(BF16)
    before, after = tops[0:4], tops[4:8]
    keep_top[0:4] = jnp.where(first, before, after)
    keep_top[4:8] = before
    send_top[0:4] = jnp.where(first, after, before)
    send_top[4:8] = before


def norm_kernel(ids, query_ref, inner_ref, carry_ref, top_ref, cols_ref, gain_ref, out_ref):
    local = pl.program_id(0)
    head = ids[0] + local
    carried = dot(query_ref[...], carry_ref[0], 1, 0)
    run = column(cols_ref, head)
    old = top_ref[pl.ds(local, 1), 0:1]
    top = jnp.maximum(run, old)
    numerator = jnp.exp(run - top) * inner_ref[...].astype(F32) + jnp.exp(old - top) * carried
    scale = lax.rsqrt(jnp.mean(numerator * numerator, axis=1, keepdims=True) + 1e-06)
    out_ref[...] = (numerator * scale * gain_ref[...]).astype(BF16)


def project_kernel(ids, near_ref, far_ref, near_weight, far_weight, out_ref):
    total = dot(near_ref[...], near_weight[...], 1, 0) + dot(far_ref[...], far_weight[...], 1, 0)
    out_ref[...] = total.astype(BF16)


def add_kernel(total_ref, far_ref, out_ref):
    out_ref[...] = (total_ref[...].astype(F32) + far_ref[...].astype(F32)).astype(BF16)


def body(conv_in, conv_weight, conv_bias, qk_weight, value_in, gate_pre, norm_gain, out_weight):
    rows = conv_in.shape[0]
    heads, keys = qk_weight.shape[1], qk_weight.shape[2]
    width = value_in.shape[1] // heads
    taps = conv_weight.shape[0]
    columns = out_weight.shape[1]
    half = heads // 2
    count = lax.axis_size("ctx")
    chips = count // 2
    per = chips // half
    part = keys // per
    me = lax.axis_index("ctx")
    core, chip = lax.rem(me, 2), me // 2
    side = lax.axis_index("head")
    keep_ids = jnp.stack([core * half, core, chip, side]).astype(jnp.int32)
    send_ids = jnp.stack([(1 - core) * half, core, chip, side]).astype(jnp.int32)

    swap = [(i, i ^ 1) for i in range(count)]
    cross = [(0, 1), (1, 0)]

    def around(distance):
        return [(i, (i + 2 * distance) % count) for i in range(count)]

    halo = lax.ppermute(conv_in[rows - TILE :], "ctx", [(i, i + 1) for i in range(count - 1)])
    rows_a, cols, sums = pl.pallas_call(
        gate_kernel,
        out_shape=(sds((2 * heads, rows), F32), sds((rows, 2 * heads), F32), sds((2 * heads, LANES), F32)),
    )(gate_pre)
    far_sums = lax.ppermute(sums, "ctx", swap)

    bias = conv_bias.reshape(1, -1)
    head_at = lambda i, ids: (0, ids[0] + i)
    local_at = lambda i, ids: (0, i)
    cols_spec = whole_block((rows, 2 * heads))

    def state_of(ids):
        return call(
            functools.partial(state_kernel, heads, keys ** -0.5),
            1,
            (half,),
            [
                pl.BlockSpec((TILE, keys), head_at),
                pl.BlockSpec((rows, keys), head_at),
                pl.BlockSpec((taps, keys), head_at),
                pl.BlockSpec((1, keys), head_at),
                pl.BlockSpec((1, 1, keys, keys), lambda i, ids: (1, ids[0] + i, 0, 0)),
                pl.BlockSpec((rows, width), head_at),
                cols_spec,
            ],
            [
                pl.BlockSpec((rows, keys), local_at),
                pl.BlockSpec((rows, keys), local_at),
                pl.BlockSpec((1, keys, width), lambda i, ids: (i, 0, 0)),
            ],
            [sds((rows, half * keys), BF16), sds((rows, half * keys), BF16), sds((half, keys, width), BF16)],
            [pltpu.VMEM((rows + 8, keys), F32)],
            cost=cost_of(2 * rows * half * keys * (keys + width), 4e6),
        )(ids, halo, conv_in, conv_weight, bias, qk_weight, value_in, cols)

    def inner_of(ids, act, key_rows):
        return call(
            inner_kernel,
            1,
            (half,),
            [
                pl.BlockSpec((rows, keys), local_at),
                pl.BlockSpec((rows, keys), local_at),
                pl.BlockSpec((1, 1, keys, keys), lambda i, ids: (0, ids[0] + i, 0, 0)),
                pl.BlockSpec((rows, width), head_at),
                whole_block((2 * heads, rows)),
                cols_spec,
            ],
            [pl.BlockSpec((rows, keys), local_at), pl.BlockSpec((rows, width), local_at)],
            [sds((rows, half * keys), BF16), sds((rows, half * width), BF16)],
            cost=cost_of(2 * rows * half * (keys * keys + rows * keys + rows * width), 4e6),
        )(ids, act, key_rows, qk_weight, value_in, rows_a, cols)

    send_act, send_keys, send_state = state_of(send_ids)
    other_state = lax.ppermute(send_state, "ctx", swap)
    keep_act, keep_keys, own_state = state_of(keep_ids)

    piece = (width // LANES * part + TILE, LANES)
    pieces = call(
        functools.partial(chip_kernel, chips, per),
        1,
        (1,),
        [whole_block((half, keys, width))] * 2 + [whole_block((2 * heads, LANES))] * 2,
        [whole_block(piece)] * chips,
        [sds(piece, BF16)] * chips,
        [pltpu.VMEM((4 * half, LANES), F32)],
    )(keep_ids, own_state, other_state, sums, far_sums)
    got = [pieces[0]] + [lax.ppermute(pieces[k], "ctx", around(k)) for k in range(1, chips)]

    send_queries, send_inner = inner_of(send_ids, send_act, send_keys)
    keep_queries, keep_inner = inner_of(keep_ids, keep_act, keep_keys)

    made = call(
        functools.partial(owner_kernel, chips),
        1,
        (1,),
        [whole_block(piece)] * chips,
        [whole_block(piece)] * chips,
        [sds(piece, BF16)] * chips,
        [pltpu.VMEM((chips,) + piece, BF16)] * 2,
    )(keep_ids, *got)
    back = [made[0]] + [lax.ppermute(made[k], "ctx", around(k)) for k in range(1, chips)]

    keep_carry, send_carry, keep_top, send_top = call(
        functools.partial(incoming_kernel, chips, per),
        1,
        (1,),
        [whole_block(piece)] * chips + [whole_block((half, keys, width))] * 2 + [whole_block((2 * heads, LANES))] * 2,
        [whole_block((half, keys, width))] * 2 + [whole_block((8, LANES))] * 2,
        [sds((half, keys, width), BF16)] * 2 + [sds((8, LANES), F32)] * 2,
        [pltpu.VMEM((8, LANES), F32)],
    )(keep_ids, *back, own_state, other_state, sums, far_sums)
    far_carry = lax.ppermute(send_carry, "ctx", swap)
    far_top = lax.ppermute(send_top, "ctx", swap)

    gain = norm_gain.reshape(1, -1)

    def normed_of(ids, queries, inner, carry, top):
        return call(
            norm_kernel,
            1,
            (half,),
            [
                pl.BlockSpec((rows, keys), local_at),
                pl.BlockSpec((rows, width), local_at),
                pl.BlockSpec((1, keys, width), lambda i, ids: (i, 0, 0)),
                whole_block((8, LANES)),
                cols_spec,
                pl.BlockSpec((1, width), head_at),
            ],
            pl.BlockSpec((rows, width), local_at),
            sds((rows, half * width), BF16),
        )(ids, queries, inner, carry, top, cols, gain)

    near = normed_of(keep_ids, keep_queries, keep_inner, keep_carry, keep_top)
    far = normed_of(send_ids, send_queries, send_inner, far_carry, far_top)

    out_columns = columns // lax.axis_size("head")
    block = 256
    depth = half * width

    def project(target, start, size):
        base = jnp.stack([core, target * (out_columns // block) + start // block]).astype(jnp.int32)
        return call(
            project_kernel,
            1,
            (size // block,),
            [
                whole_block((rows, depth)),
                whole_block((rows, depth)),
                pl.BlockSpec((depth, block), lambda i, ids: (ids[0], ids[1] + i)),
                pl.BlockSpec((depth, block), lambda i, ids: (1 - ids[0], ids[1] + i)),
            ],
            pl.BlockSpec((rows, block), lambda i, ids: (0, i)),
            sds((rows, size), BF16),
            cost=cost_of(4 * rows * depth * size, 4 * depth * size),
        )(base, near, far, out_weight, out_weight)

    sizes = [256, 768, 768, 256]
    starts = [0, 256, 1024, 1792]
    arrived = [
        lax.ppermute(project(1 - side, start, size), "head", cross) for start, size in zip(starts, sizes)
    ]
    total = project(side, 0, out_columns)
    for start, size, piece_in in zip(starts, sizes, arrived):
        first = start // block
        total = pl.pallas_call(
            add_kernel,
            grid=(size // block,),
            in_specs=[
                pl.BlockSpec((rows, block), lambda i, first=first: (0, first + i)),
                pl.BlockSpec((rows, block), lambda i: (0, i)),
            ],
            out_specs=pl.BlockSpec((rows, block), lambda i, first=first: (0, first + i)),
            out_shape=sds((rows, out_columns), BF16),
            input_output_aliases={0: 0},
        )(total, piece_in)
    return total


def solution(mesh):
    return jax.shard_map(
        body,
        mesh=mesh,
        in_specs=(
            P("ctx", "head"),
            P(None, "head"),
            P("head"),
            P(None, "head", None, None),
            P("ctx", "head"),
            P(None, "head", "ctx"),
            P("head"),
            P("head", None),
        ),
        out_specs=P("ctx", "head"),
        check_vma=False,
    )
```

```python
import functools
import jax
import jax.numpy as jnp
from jax import lax
from jax.experimental import pallas as pl
from jax.experimental.pallas import tpu as pltpu
from jax.sharding import PartitionSpec as P


F32 = jnp.float32
BF16 = jnp.bfloat16
EMPTY = -1e30
TILE = 16
LANES = 128


def dot(a, b, ca, cb):
    return lax.dot_general(a, b, (((ca,), (cb,)), ((), ())), preferred_element_type=F32)


VMEM = pl.BlockSpec(memory_space=pltpu.VMEM)
SMEM = pl.BlockSpec(memory_space=pltpu.SMEM)
ANY = pl.BlockSpec(memory_space=pl.ANY)


def call(kernel, args, out_shape, scratch=(), aliases={}, cost=None, limit=12, specs=None, out=VMEM):
    if specs is None:
        specs = [SMEM if a.dtype == jnp.int32 else VMEM for a in args]
    return pl.pallas_call(
        kernel,
        in_specs=specs,
        out_specs=jax.tree.map(lambda _: out, out_shape),
        scratch_shapes=list(scratch),
        out_shape=out_shape,
        input_output_aliases=aliases,
        cost_estimate=cost,
        compiler_params=pltpu.CompilerParams(vmem_limit_bytes=limit * 2**20),
    )(*args)


def sds(shape, dtype):
    return jax.ShapeDtypeStruct(shape, dtype)


def cost_of(flops, moved):
    return pl.CostEstimate(flops=int(flops), transcendentals=0, bytes_accessed=int(moved))


def window(index, size):
    return pl.ds(pl.multiple_of(index * size, size), size)


def gate_kernel(count, gate_hbm, *rest):
    sources, (line_ref, cols_ref, sums_ref), targets = rest[:count], rest[count : count + 3], rest[count + 3 : -3]
    gate_ref, gate_sem, sems = rest[-3:]
    first = pltpu.make_async_copy(gate_hbm, gate_ref, gate_sem)
    first.start()
    copies = [pltpu.make_async_copy(sources[i], targets[i], sems.at[i]) for i in range(count)]
    for copy in copies:
        copy.start()
    first.wait()
    gates(gate_ref, line_ref, cols_ref, sums_ref)
    for copy in copies:
        copy.wait()


def gates(gate_ref, rows_ref, cols_ref, sums_ref):
    in_gate = gate_ref[0]
    pre = gate_ref[1]
    heads, length = in_gate.shape
    log_forget = -(jnp.maximum(-pre, 0.0) + jnp.log1p(jnp.exp(-jnp.abs(pre))))
    cum = jnp.concatenate([log_forget, in_gate], axis=0)
    lane = lax.broadcasted_iota(jnp.int32, cum.shape, 1)
    step = 1
    while step < length:
        cum = cum + jnp.where(lane >= step, pltpu.roll(cum, step, 1), 0.0)
        step *= 2
    cum = cum[:heads]
    shifted = in_gate - cum
    run = jnp.concatenate([shifted, shifted], axis=0)
    rows_ref[...] = run
    step = 1
    while step < length:
        run = jnp.maximum(run, jnp.where(lane >= step, pltpu.roll(run, step, 1), -jnp.inf))
        step *= 2
    run = run[:heads]
    decay = cum[:, length - 1 :]
    top = run[:, length - 1 :]
    cols_ref[...] = jnp.transpose(jnp.concatenate([run, jnp.exp(shifted - top)], axis=0))
    sums = jnp.concatenate([top + decay, decay], axis=0)
    sums_ref[...] = jnp.broadcast_to(sums, (2 * heads, LANES))


def column(cols_ref, index):
    cols = cols_ref[...]
    lane = lax.broadcasted_iota(jnp.int32, cols.shape, 1)
    return jnp.sum(jnp.where(lane == index, cols, 0.0), axis=1, keepdims=True)


def state_kernel(keep, scale, ids, halo_ref, conv_ref, taps_ref, bias_ref, weight_ref, value_ref, cols_ref,
                 act_ref, key_ref, state_ref, pad):
    half, keys, width = state_ref.shape
    group = ids[0] if keep else 1 - ids[0]
    rows = conv_ref.shape[0]
    taps = taps_ref.shape[0]
    for local in range(half):
        head = group * half + local
        mine = window(head, keys)
        here = slice(local * keys, (local + 1) * keys)
        pad[0:8, :] = halo_ref[TILE - 8 :, mine].astype(F32)
        pad[8:, :] = conv_ref[:, mine].astype(F32)
        total = bias_ref[:, mine]
        for offset in range(taps):
            begin = 8 - (taps - 1) + offset
            total = total + taps_ref[offset : offset + 1, mine] * pad[begin : begin + rows, :]
        act = (total / (1.0 + jnp.exp(-total))).astype(BF16)
        act_ref[:, here] = act
        key_rows = (dot(act, weight_ref[1, head], 1, 0) * scale).astype(BF16)
        key_ref[:, here] = key_rows
        scaled = (key_rows.astype(F32) * column(cols_ref, 2 * half + head)).astype(BF16)
        state_ref[local] = dot(scaled, value_ref[:, window(head, width)], 0, 0).astype(BF16)


def inner_kernel(keep, ids, act_ref, key_ref, weight_ref, value_ref, rows_ref, cols_ref, query_ref, inner_ref, run_ref):
    half = act_ref.shape[1] // weight_ref.shape[2]
    keys = weight_ref.shape[2]
    width = inner_ref.shape[1] // half
    group = ids[0] if keep else 1 - ids[0]
    for local in range(half):
        head = group * half + local
        here = slice(local * keys, (local + 1) * keys)
        queries = dot(act_ref[:, here], weight_ref[0, head], 1, 0).astype(BF16)
        query_ref[:, here] = queries
        scores = dot(queries, key_ref[:, here], 1, 1)
        row = lax.broadcasted_iota(jnp.int32, scores.shape, 0)
        col = lax.broadcasted_iota(jnp.int32, scores.shape, 1)
        run = column(cols_ref, head)
        run_ref[local] = jnp.broadcast_to(run, (run.shape[0], LANES))
        log_weight = rows_ref[pl.ds(head, 1), :] - run
        weights = scores * jnp.exp(jnp.where(row >= col, log_weight, -jnp.inf))
        inner = dot(weights.astype(BF16), value_ref[:, window(head, width)], 1, 0)
        inner_ref[:, local * width : (local + 1) * width] = inner.astype(BF16)


def split_rows(value):
    high = value.astype(BF16).astype(F32)
    rest = value - high
    middle = rest.astype(BF16).astype(F32)
    return [high, middle, rest - middle]


def scalar_tile(values):
    rows = [row for value in values for row in split_rows(value)]
    rows.append(jnp.zeros((TILE - len(rows), LANES), F32))
    return jnp.concatenate(rows, axis=0).astype(BF16)


def join_rows(tile, index):
    tile = tile.astype(F32)
    return tile[3 * index : 3 * index + 1] + tile[3 * index + 1 : 3 * index + 2] + tile[3 * index + 2 : 3 * index + 3]


def wide(row, width):
    return jnp.concatenate([row] * (width // LANES), axis=1)


def place(owner, per, cut, part, span):
    block = lax.div(owner, cut)
    local = lax.div(block, per)
    row = pl.multiple_of(lax.rem(block, per) * part, part)
    lane = pl.multiple_of(lax.rem(owner, cut) * span, LANES)
    return local, row, lane


def chip_kernel(chips, sizes, ids, own_ref, other_ref, own_sums, other_sums, *rest):
    outs, weights = rest[:chips], rest[chips]
    core, chip = ids[0], ids[1]
    half = own_ref.shape[0]
    heads = 2 * half
    part, span = sizes[2], sizes[3]
    first = core == 0
    for local in range(half):
        head = core * half + local
        own_top, own_decay = own_sums[pl.ds(head, 1), :], own_sums[pl.ds(heads + head, 1), :]
        far_top, far_decay = other_sums[pl.ds(head, 1), :], other_sums[pl.ds(heads + head, 1), :]
        own_log = own_top + jnp.where(first, far_decay, 0.0)
        far_log = far_top + jnp.where(first, 0.0, own_decay)
        top = jnp.maximum(own_log, far_log)
        weights[4 * local : 4 * local + 1] = jnp.exp(own_log - top)
        weights[4 * local + 1 : 4 * local + 2] = jnp.exp(far_log - top)
        weights[4 * local + 2 : 4 * local + 3] = top
        weights[4 * local + 3 : 4 * local + 4] = own_decay + far_decay
    for k in range(chips):
        local, row, lane = place(lax.bitwise_xor(chip, k), *sizes)
        mine = weights[pl.ds(4 * local, 1), :]
        its = weights[pl.ds(4 * local + 1, 1), :]
        for b in range(span // LANES):
            lanes = pl.ds(pl.multiple_of(lane + b * LANES, LANES), LANES)
            own = own_ref[local, pl.ds(row, part), lanes].astype(F32)
            far = other_ref[local, pl.ds(row, part), lanes].astype(F32)
            outs[k][b * part : (b + 1) * part, :] = (mine * own + its * far).astype(BF16)
        outs[k][span // LANES * part :, :] = scalar_tile(
            [weights[pl.ds(4 * local + 2, 1), :], weights[pl.ds(4 * local + 3, 1), :]]
        )


def owner_kernel(chips, ids, *rest):
    ins, outs, held, made = rest[:chips], rest[chips : 2 * chips], rest[2 * chips], rest[2 * chips + 1]
    chip = ids[1]
    size = ins[0].shape[0] - TILE
    for k in range(chips):
        held[k] = ins[k][...]
    total = jnp.zeros((size, LANES), F32)
    top = jnp.full((1, LANES), EMPTY, F32)
    for source in range(chips):
        slot = lax.bitwise_xor(chip, source)
        made[slot, 0:size] = total.astype(BF16)
        made[slot, size:] = scalar_tile([top])
        if source < chips - 1:
            tile = held[slot, size:]
            new, decay = join_rows(tile, 0), join_rows(tile, 1)
            next_top = jnp.maximum(top + decay, new)
            old_weight = jnp.exp(top + decay - next_top)
            new_weight = jnp.exp(new - next_top)
            total = old_weight * total + new_weight * held[slot, 0:size].astype(F32)
            top = next_top
    for k in range(chips):
        outs[k][...] = made[k]


def incoming_kernel(chips, sizes, ids, *rest):
    ins = rest[:chips]
    own_ref, other_ref, own_sums, other_sums, keep_ref, send_ref, keep_top, send_top, tops = rest[chips:]
    core, chip = ids[0], ids[1]
    half = own_ref.shape[0]
    heads = 2 * half
    part, span = sizes[2], sizes[3]
    first = core == 0
    for k in range(chips):
        local, row, lane = place(lax.bitwise_xor(chip, k), *sizes)
        head = core * half + local
        top = join_rows(ins[k][span // LANES * part :, :], 0)
        tops[pl.ds(local, 1), :] = top
        near_top = jnp.where(first, own_sums[pl.ds(head, 1), :], other_sums[pl.ds(head, 1), :])
        near_decay = jnp.where(first, own_sums[pl.ds(heads + head, 1), :], other_sums[pl.ds(heads + head, 1), :])
        next_top = jnp.maximum(top + near_decay, near_top)
        old_weight = jnp.exp(top + near_decay - next_top)
        new_weight = jnp.exp(near_top - next_top)
        tops[pl.ds(4 + local, 1), :] = next_top
        for b in range(span // LANES):
            lanes = pl.ds(pl.multiple_of(lane + b * LANES, LANES), LANES)
            raw = ins[k][b * part : (b + 1) * part, :].astype(F32)
            own = own_ref[local, pl.ds(row, part), lanes].astype(F32)
            far = other_ref[local, pl.ds(row, part), lanes].astype(F32)
            after = old_weight * raw + new_weight * jnp.where(first, own, far)
            keep_ref[local, pl.ds(row, part), lanes] = jnp.where(first, raw, after).astype(BF16)
            send_ref[local, pl.ds(row, part), lanes] = jnp.where(first, after, raw).astype(BF16)
    before, after = tops[0:4], tops[4:8]
    keep_top[0:4] = jnp.where(first, before, after)
    keep_top[4:8] = before
    send_top[0:4] = jnp.where(first, after, before)
    send_top[4:8] = before


def norm_kernel(keep, sides, ids, *rest):
    if keep:
        query_ref, inner_ref, carry_ref, top_ref, run_ref, gain_ref, weight_ref, out_ref, chunk_ref = rest
    else:
        query_ref, inner_ref, carry_ref, top_ref, run_ref, gain_ref, weight_ref, begun_ref, out_ref, chunk_ref = rest
    half, keys, width = carry_ref.shape
    group = ids[0] if keep else 1 - ids[0]
    size = chunk_ref.shape[1]
    lanes = first_lanes(1, sides, ids, weight_ref, 0, size)
    total = None
    for local in range(half):
        head = group * half + local
        here = slice(local * width, (local + 1) * width)
        carried = dot(query_ref[:, local * keys : (local + 1) * keys], carry_ref[local], 1, 0)
        run = run_ref[local]
        old = top_ref[local : local + 1, :]
        top = jnp.maximum(run, old)
        numerator = wide(jnp.exp(run - top), width) * inner_ref[:, here].astype(F32)
        numerator = numerator + wide(jnp.exp(old - top), width) * carried
        scale = lax.rsqrt(jnp.mean(numerator * numerator, axis=1, keepdims=True) + 1e-06)
        normed = (numerator * scale * gain_ref[:, window(head, width)]).astype(BF16)
        out_ref[:, here] = normed
        part = dot(normed, weight_ref[window(head, width), lanes], 1, 0)
        total = part if total is None else total + part
    if keep:
        chunk_ref[...] = total
    else:
        chunk_ref[...] = (begun_ref[...] + total).astype(BF16)


def first_lanes(distance, sides, ids, weight_ref, start, size):
    side = lax.rem(ids[2] + distance, sides)
    return pl.ds(pl.multiple_of(side * (weight_ref.shape[1] // sides) + start, LANES), size)


def project_kernel(distance, sides, start, block, ids, near_ref, far_ref, weight_ref, out_ref):
    depth = near_ref.shape[1]
    for i in range(out_ref.shape[1] // block):
        lanes = first_lanes(distance, sides, ids, weight_ref, start + i * block, block)
        total = dot(near_ref[...], weight_ref[window(ids[0], depth), lanes], 1, 0)
        total = total + dot(far_ref[...], weight_ref[window(1 - ids[0], depth), lanes], 1, 0)
        out_ref[:, i * block : (i + 1) * block] = total.astype(BF16)


def add_kernel(start, parts, own_ref, *rest):
    total_ref, made, sem = rest[-3:]
    size = made.shape[1]
    total = own_ref[:, start : start + size].astype(F32)
    for part in rest[:parts]:
        total = total + part[...].astype(F32)
    made[...] = total.astype(BF16)
    copy = pltpu.make_async_copy(made, total_ref.at[:, start : start + size], sem)
    copy.start()
    copy.wait()


def body(conv_in, conv_weight, conv_bias, qk_weight, value_in, gate_pre, norm_gain, out_weight):
    rows = conv_in.shape[0]
    heads, keys = qk_weight.shape[1], qk_weight.shape[2]
    width = value_in.shape[1] // heads
    columns = out_weight.shape[1]
    half = heads // 2
    count = lax.axis_size("ctx")
    chips = count // 2
    cut = max(1, TILE * chips // (half * keys))
    part = half * keys * cut // chips
    sizes = (keys // part, cut, part, width // cut)
    sides = lax.axis_size("head")
    me = lax.axis_index("ctx")
    ids = jnp.stack([lax.rem(me, 2), lax.div(me, 2), lax.axis_index("head")]).astype(jnp.int32)

    swap = [(i, i ^ 1) for i in range(count)]

    def spread(made):
        came = {0: made[0]}
        for k in sorted(range(1, chips), key=lambda k: -(k & -2)):
            came[k] = lax.ppermute(made[k], "ctx", [(i, i ^ (2 * k)) for i in range(count)])
        return [came[k] for k in range(chips)]

    halo = lax.ppermute(conv_in[rows - TILE :], "ctx", [(i, i + 1) for i in range(count - 1)])
    sources = [conv_in, conv_weight, conv_bias.reshape(1, -1), qk_weight, value_in, norm_gain.reshape(1, -1)]
    line, cols, sums, conv, taps, bias, qk, values, gain = call(
        functools.partial(gate_kernel, len(sources)),
        [gate_pre, *sources],
        (sds((2 * heads, rows), F32), sds((rows, 2 * heads), F32), sds((2 * heads, LANES), F32))
        + tuple(sds(a.shape, a.dtype) for a in sources),
        [pltpu.VMEM(gate_pre.shape, F32), pltpu.SemaphoreType.DMA, pltpu.SemaphoreType.DMA((len(sources),))],
        specs=[ANY] * (1 + len(sources)),
    )
    far_sums = lax.ppermute(sums, "ctx", swap)

    def state_of(keep):
        return call(
            functools.partial(state_kernel, keep, keys ** -0.5),
            [ids, halo, conv, taps, bias, qk, values, cols],
            (sds((rows, half * keys), BF16), sds((rows, half * keys), BF16), sds((half, keys, width), BF16)),
            [pltpu.VMEM((rows + 8, keys), F32)],
        )

    def inner_of(keep, act, key_rows):
        return call(
            functools.partial(inner_kernel, keep),
            [ids, act, key_rows, qk, values, line, cols],
            (sds((rows, half * keys), BF16), sds((rows, half * width), BF16), sds((half, rows, LANES), F32)),
            cost=cost_of(2 * rows * half * (keys * keys + rows * keys + rows * width), 4e6),
        )

    send_act, send_keys, send_state = state_of(False)
    other_state = lax.ppermute(send_state, "ctx", swap)
    keep_act, keep_keys, own_state = state_of(True)

    piece = sds((width // cut // LANES * part + TILE, LANES), BF16)
    pieces = call(
        functools.partial(chip_kernel, chips, sizes),
        [ids, own_state, other_state, sums, far_sums],
        (piece,) * chips,
        [pltpu.VMEM((4 * half, LANES), F32)],
    )
    got = spread(pieces)
    send_act, send_keys, _ = lax.optimization_barrier((send_act, send_keys, pieces[0]))
    send_queries, send_inner, send_run = inner_of(False, send_act, send_keys)
    got[0], send_inner = lax.optimization_barrier((got[0], send_inner))

    made = call(
        functools.partial(owner_kernel, chips),
        [ids, *got],
        (piece,) * chips,
        [pltpu.VMEM((chips,) + piece.shape, BF16)] * 2,
    )
    back = spread(made)
    keep_act, keep_keys, _ = lax.optimization_barrier((keep_act, keep_keys, made[0]))
    keep_queries, keep_inner, keep_run = inner_of(True, keep_act, keep_keys)
    back[0], keep_inner = lax.optimization_barrier((back[0], keep_inner))

    state_shape = sds((half, keys, width), BF16)
    keep_carry, send_carry, keep_top, send_top = call(
        functools.partial(incoming_kernel, chips, sizes),
        [ids, *back, own_state, other_state, sums, far_sums],
        (state_shape, state_shape, sds((8, LANES), F32), sds((8, LANES), F32)),
        [pltpu.VMEM((8, LANES), F32)],
    )
    far_carry = lax.ppermute(send_carry, "ctx", swap)
    far_top = lax.ppermute(send_top, "ctx", swap)

    block = 256
    near, begun = call(
        functools.partial(norm_kernel, True, sides),
        [ids, keep_queries, keep_inner, keep_carry, keep_top, keep_run, gain, out_weight],
        (sds((rows, half * width), BF16), sds((rows, block), F32)),
    )
    far, first = call(
        functools.partial(norm_kernel, False, sides),
        [ids, send_queries, send_inner, far_carry, far_top, send_run, gain, out_weight, begun],
        (sds((rows, half * width), BF16), sds((rows, block), BF16)),
    )

    out_columns = columns // sides

    def project(distance, start, size):
        return call(
            functools.partial(project_kernel, distance, sides, start, block),
            [ids, near, far, out_weight],
            sds((rows, size), BF16),
            cost=cost_of(4 * rows * half * width * size, 4 * half * width * size),
        )

    blocks = out_columns // block
    cuts = [0, 1, 1 + (blocks - 2) // 2, blocks - 1, blocks]
    chunks = [(low * block, (high - low) * block) for low, high in zip(cuts, cuts[1:])]
    arrived = {}
    for index in range(len(chunks) * (sides - 1)):
        start, size = chunks[index // (sides - 1)]
        distance = 1 + index % (sides - 1)
        value = first
        if index > 0:
            value = project(distance, start, size)
        came = lax.ppermute(value, "head", [(i, (i + distance) % sides) for i in range(sides)])
        arrived.setdefault((start, size), []).append(came)
    own = project(0, 0, out_columns)
    total = []
    for (start, size), parts in arrived.items():
        total = [
            call(
                functools.partial(add_kernel, start, len(parts)),
                [own, *parts, *total],
                sds((rows, out_columns), BF16),
                [pltpu.VMEM((rows, size), BF16), pltpu.SemaphoreType.DMA],
                aliases={1 + len(parts): 0} if total else {},
                specs=[VMEM] * (1 + len(parts)) + [ANY] * len(total),
                out=ANY,
            )
        ]
    return total[0]


def solution(mesh):
    return jax.shard_map(
        body,
        mesh=mesh,
        in_specs=(
            P("ctx", "head"),
            P(None, "head"),
            P("head"),
            P(None, "head", None, None),
            P("ctx", "head"),
            P(None, "head", "ctx"),
            P("head"),
            P("head", None),
        ),
        out_specs=P("ctx", "head"),
        check_vma=False,
    )
```
